32 devices in a mesh: dp: 8 (over z, x), row: 2 (over y), col: 2 (over core).
Axes of the slice: x: 2, y: 2, z: 4, core: 2. Of those that a mesh axis runs over, the one named last changes fastest.
Arguments:
- block_in: float32 [8192, 768], P(('dp', 'row'), 'col'), may hold values from -6 to 6
- upstream: float32 [8192, 768], P(('dp', 'row'), 'col'), may hold values from -6 to 6
- norm_params: float32 [4, 768], P(None, 'col'), may hold values from -0.5 to 1.5
- w_qkv: float32 [3, 12, 64, 768], P(None, 'row', 'dp', 'col'), may hold values from -1.4433757 to 1.4433757
- w_attn: float32 [12, 64, 768], P('row', 'dp', 'col'), may hold values from -0.875 to 0.875
- w_up: float32 [3072, 768], P(('dp', 'row'), 'col'), may hold values from -0.21875 to 0.21875
- w_down: float32 [3072, 768], P(('dp', 'row'), 'col'), may hold values from -0.109375 to 0.109375
- mom_norm: float32 [2, 4, 768], P(None, None, 'col'), may hold values from -0.224 to 0.224, as said below
- mom_qkv: float32 [2, 3, 12, 64, 768], P(None, None, 'row', 'dp', 'col'), may hold values from -0.16 to 0.16, as said below
- mom_attn: float32 [2, 12, 64, 768], P(None, 'row', 'dp', 'col'), may hold values from -0.048 to 0.048, as said below
- mom_up: float32 [2, 3072, 768], P(None, ('dp', 'row'), 'col'), may hold values from -0.128 to 0.128, as said below
- mom_down: float32 [2, 3072, 768], P(None, ('dp', 'row'), 'col'), may hold values from -0.208 to 0.208, as said below
Outputs:
- block_out: float32 [8192, 768], P(('dp', 'row'), 'col')
- input_grad: float32 [8192, 768], P(('dp', 'row'), 'col')
- grad_norm: float32 [4, 768], P(None, 'col')
- grad_qkv: float32 [3, 12, 64, 768], P(None, 'row', 'dp', 'col')
- grad_attn: float32 [12, 64, 768], P('row', 'dp', 'col')
- grad_up: float32 [3072, 768], P(('dp', 'row'), 'col')
- grad_down: float32 [3072, 768], P(('dp', 'row'), 'col')
- new_norm: float32 [4, 768], P(None, 'col')
- new_qkv: float32 [3, 12, 64, 768], P(None, 'row', 'dp', 'col')
- new_attn: float32 [12, 64, 768], P('row', 'dp', 'col')
- new_up: float32 [3072, 768], P(('dp', 'row'), 'col')
- new_down: float32 [3072, 768], P(('dp', 'row'), 'col')
- new_mom_norm: float32 [2, 4, 768], P(None, None, 'col')
- new_mom_qkv: float32 [2, 3, 12, 64, 768], P(None, None, 'row', 'dp', 'col')
- new_mom_attn: float32 [2, 12, 64, 768], P(None, 'row', 'dp', 'col')
- new_mom_up: float32 [2, 3072, 768], P(None, ('dp', 'row'), 'col')
- new_mom_down: float32 [2, 3072, 768], P(None, ('dp', 'row'), 'col')
The draws below stay inside these ranges and needn't reach their ends.
Inputs may be any that keep to these rules, and one draw needn't show every extreme that they name: `mom_norm`: second moments are positive. `mom_qkv`: second moments are positive. `mom_attn`: second moments are positive. `mom_up`: second moments are positive. `mom_down`: second moments are positive.
All inputs are finite; a program needn't handle non-finite values.
Results may differ from the reference program's by a relative error of at most 0.012.
The reference program's roundings to bfloat16 on the way count: a program that leaves them out, or rounds other values in their place, can miss the bound.
Values may be sent and summed in bfloat16 or wider, within the bound.
A program may use at most 128 MiB of HBM per device.

```python
import math
import jax
import jax.numpy as jnp
from jax import lax

D = 768
H = 12
HD = 64
FF = 3072
SEQ = 512
STEP = 4
TOKENS = 8192


def draw_norm_params(key, part):
    gain_rows = jax.random.uniform(jax.random.fold_in(key, 1), (2, D), jnp.float32, 0.7, 1.3)
    shifts = jax.random.uniform(jax.random.fold_in(key, 2), (2, D), jnp.float32, -0.3, 0.3)
    return jnp.stack([gain_rows[0], shifts[0], gain_rows[1], shifts[1]])


def draw_w_qkv(key, part):
    base_draw = jnp.clip(jax.random.normal(jax.random.fold_in(key, 3), (3, H, HD, D), jnp.float32), -5.0, 5.0)
    base_draw = base_draw / math.sqrt(D)
    query_lift = jnp.array([1.5, 1.0, 1.0], jnp.float32)
    drawn_draw = base_draw * query_lift[:, None, None, None]
    return drawn_draw


def moment_pair(key, shape, grad_size):
    log_low = math.log(0.005)
    log_high = math.log(0.05)
    first_moment = grad_size * 0.08 * jnp.clip(jax.random.normal(jax.random.fold_in(key, 21), shape, jnp.float32), -4.0, 4.0)
    second_moment = grad_size * grad_size * jnp.exp(jax.random.uniform(jax.random.fold_in(key, 22), shape, jnp.float32, log_low, log_high))
    return jnp.stack([first_moment, second_moment])


def draw_mom_norm(key, part):
    return moment_pair(key, (4, D), 0.7)


def draw_mom_qkv(key, part):
    return moment_pair(key, (3, H, HD, D), 0.5)


def draw_mom_attn(key, part):
    return moment_pair(key, (H, HD, D), 0.15)


def draw_mom_up(key, part):
    return moment_pair(key, (FF, D), 0.4)


def draw_mom_down(key, part):
    return moment_pair(key, (FF, D), 0.65)


def shard_levels(rng, dims, shards, smallest, high):
    def one(position, blocks):
        heights = jax.random.uniform(jax.random.fold_in(jax.random.fold_in(rng, 6), position), (blocks,), jnp.float32, smallest / len(shards), high / len(shards))
        return jnp.repeat(jnp.exp(heights), dims[position] // blocks).reshape((-1,) + (1,) * (len(dims) - position - 1))

    gain = one(*shards[0])
    for cut in shards[1:]:
        gain = gain * one(*cut)
    return gain


def normal_values(rng, dims, scale, reach, split=(), kind=jnp.bfloat16):
    result = scale * jax.random.normal(rng, dims, jnp.float32)
    if split:
        result = result * shard_levels(rng, dims, split, -0.22, 0.18)
    return jnp.clip(result, -reach, reach).astype(kind)


def setup_inputs(seed: int = 0) -> dict:
    key_of = jax.random.split(jax.random.key(seed), 13)
    block_in = normal_values(key_of[0], (TOKENS, D), 1.0, 6.0, ((0, 16), (1, 2)), jnp.float32)
    upstream = normal_values(key_of[1], (TOKENS, D), 1.0, 6.0, ((0, 16), (1, 2)), jnp.float32)
    norm_params = draw_norm_params(jax.random.fold_in(key_of[12], 71), 0)
    w_qkv = draw_w_qkv(jax.random.fold_in(key_of[12], 71), 0)
    w_attn = normal_values(key_of[4], (H, HD, D), (D // 16) ** -0.5, 0.875, ((0, 2), (1, 8), (2, 2)), jnp.float32)
    w_up = normal_values(key_of[5], (FF, D), D ** -0.5, 0.21875, ((0, 16), (1, 2)), jnp.float32)
    w_down = normal_values(key_of[6], (FF, D), FF ** -0.5, 0.109375, ((0, 16), (1, 2)), jnp.float32)
    mom_norm = draw_mom_norm(jax.random.fold_in(key_of[12], 71), 0)
    mom_qkv = draw_mom_qkv(jax.random.fold_in(key_of[12], 71), 0)
    mom_attn = draw_mom_attn(jax.random.fold_in(key_of[12], 71), 0)
    mom_up = draw_mom_up(jax.random.fold_in(key_of[12], 71), 0)
    mom_down = draw_mom_down(jax.random.fold_in(key_of[12], 71), 0)
    return {"block_in": block_in, "upstream": upstream, "norm_params": norm_params, "w_qkv": w_qkv, "w_attn": w_attn, "w_up": w_up, "w_down": w_down, "mom_norm": mom_norm, "mom_qkv": mom_qkv, "mom_attn": mom_attn, "mom_up": mom_up, "mom_down": mom_down}


norm_eps = 1e-05
adam_eps = 1e-08
beta_one = 0.9
beta_two = 0.95
learn_rate = 0.02
decay_rate = 0.1
gelu_coef = math.sqrt(2.0 / math.pi)
cubic_coef = 0.044715
masked_score = -1e+30

def layer_norm(rows_in, gain_row, shift_row):
    center = rows_in - lax.optimization_barrier(jnp.mean(rows_in, axis=1, keepdims=True))
    spread = lax.optimization_barrier(jnp.mean(center * center, axis=1, keepdims=True))
    inverse = lax.rsqrt(spread + norm_eps)
    normal = center * inverse
    return (normal, inverse, (normal * gain_row + shift_row).astype(jnp.bfloat16))

def norm_back(grad_normed, normal, inverse, gain_row):
    scaled = grad_normed * gain_row
    first_mean = lax.optimization_barrier(jnp.mean(scaled, axis=1, keepdims=True))
    second_mean = lax.optimization_barrier(jnp.mean(scaled * normal, axis=1, keepdims=True))
    return inverse * (scaled - first_mean - normal * second_mean)

def smooth_pair(values):
    squared = values * values
    bent = jnp.tanh(gelu_coef * (values + cubic_coef * squared * values))
    smooth = 0.5 * values * (1.0 + bent)
    slope = 0.5 * (1.0 + bent) + 0.5 * values * (1.0 - bent * bent) * gelu_coef * (1.0 + 3.0 * cubic_coef * squared)
    return (smooth, slope)

def causal_mask(length):
    return lax.broadcasted_iota(jnp.int32, (length, length), 0) >= lax.broadcasted_iota(jnp.int32, (length, length), 1)

def seq_scores(qkv_seq):
    score_scale = 1.0 / math.sqrt(qkv_seq.shape[3])
    q_rows = qkv_seq[:, 0].astype(jnp.float32)
    k_rows = qkv_seq[:, 1].astype(jnp.float32)
    scores = jnp.einsum('qhd,khd->hqk', q_rows, k_rows) * score_scale
    return (jnp.where(causal_mask(qkv_seq.shape[0])[None], scores, masked_score), score_scale)

def attend(qkv_seq):
    scores, score_scale = seq_scores(qkv_seq)
    highest = lax.optimization_barrier(jnp.max(scores, axis=2, keepdims=True))
    log_total = highest + jnp.log(lax.optimization_barrier(jnp.sum(jnp.exp(scores - highest), axis=2, keepdims=True)))
    attn_probs = jnp.exp(scores - log_total).astype(jnp.bfloat16)
    mixed = jnp.einsum('hqk,khd->qhd', attn_probs.astype(jnp.float32), qkv_seq[:, 2].astype(jnp.float32))
    return (mixed.astype(jnp.bfloat16).reshape(qkv_seq.shape[0], -1), log_total)

def attend_back(qkv_seq, grad_mixed, log_total):
    grad_mixed = grad_mixed.reshape(qkv_seq.shape[0], qkv_seq.shape[2], qkv_seq.shape[3]).astype(jnp.float32)
    scores, score_scale = seq_scores(qkv_seq)
    attn_probs = jnp.exp(scores - log_total)
    probs_b = attn_probs.astype(jnp.bfloat16).astype(jnp.float32)
    q_rows = qkv_seq[:, 0].astype(jnp.float32)
    k_rows = qkv_seq[:, 1].astype(jnp.float32)
    v_rows = qkv_seq[:, 2].astype(jnp.float32)
    grad_values = jnp.einsum('hqk,qhd->khd', probs_b, grad_mixed)
    grad_probs = jnp.einsum('qhd,khd->hqk', grad_mixed, v_rows)
    delta_rows = lax.optimization_barrier(jnp.sum(attn_probs * grad_probs, axis=2, keepdims=True))
    grad_scores = (attn_probs * (grad_probs - delta_rows) * score_scale).astype(jnp.bfloat16).astype(jnp.float32)
    grad_queries = jnp.einsum('hqk,khd->qhd', grad_scores, k_rows)
    grad_keys = jnp.einsum('hqk,qhd->khd', grad_scores, q_rows)
    return jnp.stack([grad_queries, grad_keys, grad_values], axis=1).astype(jnp.bfloat16)

def adam_step(weight, grad, moments, decay):
    first_moment = beta_one * moments[0] + (1.0 - beta_one) * grad
    second_moment = beta_two * moments[1] + (1.0 - beta_two) * grad * grad
    step_size = first_moment / (1.0 - beta_one ** STEP) / (jnp.sqrt(second_moment / (1.0 - beta_two ** STEP)) + adam_eps)
    return (weight - learn_rate * (step_size + decay * weight), jnp.stack([first_moment, second_moment]))

def reference(block_in, upstream, norm_params, w_qkv, w_attn, w_up, w_down, mom_norm, mom_qkv, mom_attn, mom_up, mom_down):
    qkv_mat = w_qkv.reshape(3 * D, D).astype(jnp.bfloat16)
    attn_mat = w_attn.reshape(D, D).astype(jnp.bfloat16)
    up_mat = w_up.astype(jnp.bfloat16)
    down_mat = w_down.astype(jnp.bfloat16)
    seq_total = TOKENS // SEQ
    per_block = math.gcd(seq_total, 8)
    block_rows = per_block * SEQ

    def one_block(carry, block_index):
        first_row = (block_index * block_rows).astype(jnp.int32)
        rows_in = lax.dynamic_slice_in_dim(block_in, first_row, block_rows, 0)
        rows_up = lax.dynamic_slice_in_dim(upstream, first_row, block_rows, 0)
        normal_one, inverse_one, normed_one = layer_norm(rows_in, norm_params[0], norm_params[1])
        triples = jnp.dot(normed_one, qkv_mat.T, preferred_element_type=jnp.float32).astype(jnp.bfloat16)
        triples = triples.reshape(per_block, SEQ, 3, H, HD)
        mixed, log_total = jax.vmap(attend)(triples)
        mixed_rows = mixed.reshape(block_rows, D)
        middle = rows_in + jnp.dot(mixed_rows, attn_mat, preferred_element_type=jnp.float32)
        normal_two, inverse_two, normed_two = layer_norm(middle, norm_params[2], norm_params[3])
        hidden_pre = jnp.dot(normed_two, up_mat.T, preferred_element_type=jnp.float32)
        activated, slope = smooth_pair(hidden_pre)
        activated = activated.astype(jnp.bfloat16)
        block_out = middle + jnp.dot(activated, down_mat, preferred_element_type=jnp.float32)
        upstream_b = rows_up.astype(jnp.bfloat16)
        grad_hidden = jnp.dot(upstream_b, down_mat.T, preferred_element_type=jnp.float32)
        grad_pre = (grad_hidden * slope).astype(jnp.bfloat16)
        grad_normed_two = jnp.dot(grad_pre, up_mat, preferred_element_type=jnp.float32)
        middle_grad = rows_up + norm_back(grad_normed_two, normal_two, inverse_two, norm_params[2])
        middle_b = middle_grad.astype(jnp.bfloat16)
        grad_mixed = jnp.dot(middle_b, attn_mat.T, preferred_element_type=jnp.float32).astype(jnp.bfloat16)
        grad_mixed = grad_mixed.reshape(per_block, SEQ, D)
        grad_triples = jax.vmap(attend_back)(triples, grad_mixed, log_total).reshape(block_rows, 3 * D)
        grad_normed_one = jnp.dot(grad_triples, qkv_mat, preferred_element_type=jnp.float32)
        input_grad = middle_grad + norm_back(grad_normed_one, normal_one, inverse_one, norm_params[0])
        norm_terms = jnp.stack([lax.optimization_barrier(jnp.sum(grad_normed_one * normal_one, axis=0)), lax.optimization_barrier(jnp.sum(grad_normed_one, axis=0)), lax.optimization_barrier(jnp.sum(grad_normed_two * normal_two, axis=0)), lax.optimization_barrier(jnp.sum(grad_normed_two, axis=0))])
        totals = (carry[0] + jnp.dot(grad_triples.T, normed_one, preferred_element_type=jnp.float32), carry[1] + jnp.dot(mixed_rows.T, middle_b, preferred_element_type=jnp.float32), carry[2] + jnp.dot(grad_pre.T, normed_two, preferred_element_type=jnp.float32), carry[3] + jnp.dot(activated.T, upstream_b, preferred_element_type=jnp.float32), carry[4] + norm_terms)
        return (totals, (block_out, input_grad))
    start_totals = (jnp.zeros((3 * D, D), jnp.float32), jnp.zeros((D, D), jnp.float32), jnp.zeros((FF, D), jnp.float32), jnp.zeros((FF, D), jnp.float32), jnp.zeros((4, D), jnp.float32))
    totals, (outs_all, grads_all) = lax.scan(one_block, start_totals, jnp.arange(seq_total // per_block, dtype=jnp.int32))
    factor = 1.0 / math.sqrt(TOKENS)
    grad_qkv = (totals[0] * factor).reshape(3, H, HD, D)
    grad_attn = (totals[1] * factor).reshape(H, HD, D)
    grad_up = totals[2] * factor
    grad_down = totals[3] * factor
    grad_norm = totals[4] * factor
    new_norm, new_mom_norm = adam_step(norm_params, grad_norm, mom_norm, 0.0)
    new_qkv, new_mom_qkv = adam_step(w_qkv, grad_qkv, mom_qkv, decay_rate)
    new_attn, new_mom_attn = adam_step(w_attn, grad_attn, mom_attn, decay_rate)
    new_up, new_mom_up = adam_step(w_up, grad_up, mom_up, decay_rate)
    new_down, new_mom_down = adam_step(w_down, grad_down, mom_down, decay_rate)
    block_out = outs_all.reshape(TOKENS, D)
    input_grad = grads_all.reshape(TOKENS, D)
    return (block_out, input_grad, grad_norm, grad_qkv, grad_attn, grad_up, grad_down, new_norm, new_qkv, new_attn, new_up, new_down, new_mom_norm, new_mom_qkv, new_mom_attn, new_mom_up, new_mom_down)
```

```python
import functools
import math

import jax
import jax.numpy as jnp
from jax import lax
from jax.experimental import pallas as pl
from jax.experimental.pallas import tpu as pltpu
from jax.sharding import PartitionSpec as P

SEQ = 512
STEP = 4
LOW = 2


norm_eps = 1e-05
adam_eps = 1e-08
beta_one = 0.9
beta_two = 0.95
learn_rate = 0.02
decay_rate = 0.1
gelu_coef = math.sqrt(2.0 / math.pi)
cubic_coef = 0.044715
masked_score = -1e30

group = ("row", "col")
swap_pair = [(0, 1), (1, 0)]
spread_first = [(1, 2), (2, 1)]
spread_second = [(0, 2), (3, 1), (1, 0), (2, 3)]
collect_second = [(dst, src) for src, dst in spread_second]


def smooth_pair(values):
    squared = values * values
    bent = jnp.tanh(gelu_coef * (values + cubic_coef * squared * values))
    smooth = 0.5 * values * (1.0 + bent)
    slope = 0.5 * (1.0 + bent) + 0.5 * values * (1.0 - bent * bent) * gelu_coef * (
        1.0 + 3.0 * cubic_coef * squared
    )
    return (smooth, slope)


def wide(left, right, dims):
    return lax.dot_general(left, right, (dims, ((), ())), preferred_element_type=jnp.float32)


def normalize(rows_in, gain_row, shift_row):
    count = rows_in.shape[1]
    mean_here = jnp.mean(rows_in, axis=1, keepdims=True)
    offset = rows_in - mean_here
    square_here = jnp.sum(offset * offset, axis=1, keepdims=True)
    there = lax.ppermute(jnp.concatenate([mean_here, square_here], axis=1), "col", swap_pair)
    gap = mean_here - there[:, :1]
    spread = (square_here + there[:, 1:] + gap * gap * (0.5 * count)) / (2.0 * count)
    inverse = lax.rsqrt(spread + norm_eps)
    normal = (rows_in - (mean_here - 0.5 * gap)) * inverse
    return (normal, inverse, (normal * gain_row + shift_row).astype(jnp.bfloat16))


def norm_back(grad_normed, normal, inverse, gain_row):
    count = 2.0 * grad_normed.shape[1]
    scaled = grad_normed * gain_row
    here = jnp.concatenate(
        [
            jnp.sum(scaled, axis=1, keepdims=True),
            jnp.sum(scaled * normal, axis=1, keepdims=True),
        ],
        axis=1,
    )
    total = (here + lax.ppermute(here, "col", swap_pair)) / count
    return inverse * (scaled - total[:, :1] - normal * total[:, 1:])


def pick(flag, one, other):
    return jnp.where(flag, one, other), jnp.where(flag, other, one)


def spread_rows(block):
    row, col = lax.axis_index("row"), lax.axis_index("col")
    first = lax.ppermute(block, group, spread_first)
    second = lax.ppermute(block, group, spread_second)
    first = jnp.where(row == col, block, first)
    low, high = pick(row == 0, first, second)
    return low, high


def collect_rows(low, high):
    row, col = lax.axis_index("row"), lax.axis_index("col")
    first, second = pick(row == 0, low, high)
    first_in = lax.ppermute(first.astype(jnp.bfloat16), group, spread_first)
    second_in = lax.ppermute(second.astype(jnp.bfloat16), group, collect_second)
    return jnp.where(row == col, first, first_in.astype(jnp.float32)) + second_in.astype(
        jnp.float32
    )


def out_project(rows, weight):
    half = weight.shape[1] // 2
    return collect_rows(
        wide(rows, weight[:, :half], ((1,), (0,))), wide(rows, weight[:, half:], ((1,), (0,)))
    )


def small_ring():
    size = lax.axis_size("dp")
    return size % LOW == 0 and size <= 8


def high_steps(sign):
    size = lax.axis_size("dp")
    high = size // LOW
    return [
        [(i, ((i // LOW + sign * step) % high) * LOW + i % LOW) for i in range(size)]
        for step in range(1, high)
    ]


def low_step():
    return [(i, i ^ 1) for i in range(lax.axis_size("dp"))]


def gather_weight(shard, axis):
    shard = shard.astype(jnp.bfloat16)
    if small_ring():
        near = jnp.concatenate(
            [shard] + [lax.ppermute(shard, "dp", perm) for perm in high_steps(1)], axis=axis
        )
        block = jnp.concatenate([near, lax.ppermute(near, "dp", low_step())], axis=axis)
    else:
        block = lax.all_gather(shard, "dp", axis=axis, tiled=True)
    there = lax.ppermute(block, "col", swap_pair)
    low, high = pick(lax.axis_index("col") == 0, block, there)
    return jnp.concatenate([low, high], axis=-1)


def reduce_weight(make, axis):
    away = make(False).astype(jnp.bfloat16)
    total = make(True) + lax.ppermute(away, "col", swap_pair).astype(jnp.float32)
    if not small_ring():
        return lax.psum_scatter(total, "dp", scatter_dimension=axis, tiled=True)
    near, far = jnp.split(total, 2, axis=axis)
    near = near + lax.ppermute(far.astype(jnp.bfloat16), "dp", low_step()).astype(jnp.float32)
    own, *rest = jnp.split(near, lax.axis_size("dp") // LOW, axis=axis)
    for piece, perm in zip(rest, high_steps(-1)):
        own = own + lax.ppermute(piece.astype(jnp.bfloat16), "dp", perm).astype(jnp.float32)
    return own


def sum_everywhere(terms):
    if not small_ring():
        return lax.psum(terms, ("dp", "row"))
    terms = terms + lax.ppermute(terms, "row", swap_pair)
    terms = terms + lax.ppermute(terms, "dp", low_step())
    moved = [lax.ppermute(terms, "dp", perm) for perm in high_steps(1)]
    for piece in moved:
        terms = terms + piece
    return terms


def head_scores(triples_ref, heads, size, head):
    width = heads * size
    query = triples_ref[:, head * size : (head + 1) * size]
    key = triples_ref[:, width + head * size : width + (head + 1) * size]
    value = triples_ref[:, 2 * width + head * size : 2 * width + (head + 1) * size]
    scores = wide(query, key, ((1,), (1,))) * (1.0 / math.sqrt(size))
    length = scores.shape[0]
    allowed = lax.broadcasted_iota(jnp.int32, (length, length), 0) >= lax.broadcasted_iota(
        jnp.int32, (length, length), 1
    )
    return query, key, value, jnp.where(allowed, scores, masked_score)


def attend_kernel(heads, size, triples_ref, mixed_ref, total_ref):
    for head in range(heads):
        _, _, value, scores = head_scores(triples_ref, heads, size, head)
        highest = jnp.max(scores, axis=1, keepdims=True)
        log_total = highest + jnp.log(jnp.sum(jnp.exp(scores - highest), axis=1, keepdims=True))
        probs = jnp.exp(scores - log_total).astype(jnp.bfloat16)
        mixed_ref[:, head * size : (head + 1) * size] = wide(probs, value, ((1,), (0,))).astype(
            jnp.bfloat16
        )
        total_ref[:, head : head + 1] = log_total


def attend_back_kernel(heads, size, triples_ref, grad_ref, total_ref, out_ref):
    width = heads * size
    scale = 1.0 / math.sqrt(size)
    for head in range(heads):
        query, key, value, scores = head_scores(triples_ref, heads, size, head)
        grad_mixed = grad_ref[:, head * size : (head + 1) * size]
        probs = jnp.exp(scores - total_ref[:, head : head + 1])
        grad_values = wide(probs.astype(jnp.bfloat16), grad_mixed, ((0,), (0,)))
        grad_probs = wide(grad_mixed, value, ((1,), (1,)))
        delta = jnp.sum(probs * grad_probs, axis=1, keepdims=True)
        grad_scores = (probs * (grad_probs - delta) * scale).astype(jnp.bfloat16)
        for part, piece in enumerate(
            (
                wide(grad_scores, key, ((1,), (0,))),
                wide(grad_scores, query, ((0,), (0,))),
                grad_values,
            )
        ):
            start = part * width + head * size
            out_ref[:, start : start + size] = piece.astype(jnp.bfloat16)


def by_sequence(kernel, operands, outs):
    rows = operands[0].shape[0]

    def spec(shape):
        return pl.BlockSpec((SEQ, shape[1]), lambda step: (step, 0))

    return pl.pallas_call(
        kernel,
        grid=(rows // SEQ,),
        in_specs=[spec(item.shape) for item in operands],
        out_specs=[spec(item.shape) for item in outs],
        out_shape=outs,
        compiler_params=pltpu.CompilerParams(vmem_limit_bytes=40 * 1024 * 1024),
        cost_estimate=pl.CostEstimate(
            flops=rows * SEQ * 2048, bytes_accessed=rows * 8192, transcendentals=rows * SEQ * 6
        ),
    )(*operands)


def adam_step(weight, grad, moments, decay):
    first_moment = beta_one * moments[0] + (1.0 - beta_one) * grad
    second_moment = beta_two * moments[1] + (1.0 - beta_two) * grad * grad
    step_size = (
        first_moment
        / (1.0 - beta_one**STEP)
        / (jnp.sqrt(second_moment / (1.0 - beta_two**STEP)) + adam_eps)
    )
    return (
        weight - learn_rate * (step_size + decay * weight),
        jnp.stack([first_moment, second_moment]),
    )


def on_device(
    block_in,
    upstream,
    norm_params,
    w_qkv,
    w_attn,
    w_up,
    w_down,
    mom_norm,
    mom_qkv,
    mom_attn,
    mom_up,
    mom_down,
):
    heads = w_qkv.shape[1]
    size = w_qkv.shape[2] * lax.axis_size("dp")
    width = heads * size
    at_low = lax.axis_index("col") == 0

    normal_one, inverse_one, normed_one = normalize(block_in, norm_params[0], norm_params[1])
    qkv_mat = gather_weight(w_qkv, 2).reshape(3 * width, -1)
    one_low, one_high = spread_rows(normed_one)
    attn_mat = gather_weight(w_attn, 1).reshape(width, -1)
    up_mat = gather_weight(w_up, 0)
    up_low, up_high = spread_rows(upstream.astype(jnp.bfloat16))
    down_mat = gather_weight(w_down, 0)

    triples = wide(
        jnp.concatenate([one_low, one_high], axis=1), qkv_mat, ((1,), (1,))
    ).astype(jnp.bfloat16)
    mixed, log_total = by_sequence(
        functools.partial(attend_kernel, heads, size),
        (triples,),
        (
            jax.ShapeDtypeStruct((triples.shape[0], width), jnp.bfloat16),
            jax.ShapeDtypeStruct((triples.shape[0], heads), jnp.float32),
        ),
    )
    middle = block_in + out_project(mixed, attn_mat)
    normal_two, inverse_two, normed_two = normalize(middle, norm_params[2], norm_params[3])
    two_low, two_high = spread_rows(normed_two)
    grad_hidden = wide(jnp.concatenate([up_low, up_high], axis=1), down_mat, ((1,), (1,)))
    hidden_pre = wide(jnp.concatenate([two_low, two_high], axis=1), up_mat, ((1,), (1,)))
    activated, slope = smooth_pair(hidden_pre)
    activated = activated.astype(jnp.bfloat16)
    grad_pre = (grad_hidden * slope).astype(jnp.bfloat16)
    grad_normed_two = out_project(grad_pre, up_mat)
    block_out = middle + out_project(activated, down_mat)

    def products(left, low, high):
        own, away = pick(at_low, low, high)
        return lambda mine: wide(left, own if mine else away, ((0,), (0,)))

    grad_down = reduce_weight(products(activated, up_low, up_high), 0)
    grad_up = reduce_weight(products(grad_pre, two_low, two_high), 0)
    middle_grad = upstream + norm_back(grad_normed_two, normal_two, inverse_two, norm_params[2])
    mid_low, mid_high = spread_rows(middle_grad.astype(jnp.bfloat16))
    grad_mixed = wide(
        jnp.concatenate([mid_low, mid_high], axis=1), attn_mat, ((1,), (1,))
    ).astype(jnp.bfloat16)

    def by_head(make, parts):
        return lambda mine: make(mine).reshape(*parts, heads, size, -1)

    grad_attn = reduce_weight(by_head(products(mixed, mid_low, mid_high), ()), 1)
    (grad_triples,) = by_sequence(
        functools.partial(attend_back_kernel, heads, size),
        (triples, grad_mixed, log_total),
        (jax.ShapeDtypeStruct(triples.shape, jnp.bfloat16),),
    )
    grad_qkv = reduce_weight(by_head(products(grad_triples, one_low, one_high), (3,)), 2)
    grad_normed_one = out_project(grad_triples, qkv_mat)
    input_grad = middle_grad + norm_back(grad_normed_one, normal_one, inverse_one, norm_params[0])
    norm_terms = jnp.stack(
        [
            jnp.sum(grad_normed_one * normal_one, axis=0),
            jnp.sum(grad_normed_one, axis=0),
            jnp.sum(grad_normed_two * normal_two, axis=0),
            jnp.sum(grad_normed_two, axis=0),
        ]
    )
    grad_norm = sum_everywhere(norm_terms)
    token_count = block_in.shape[0] * lax.axis_size("dp") * lax.axis_size("row")
    factor = 1.0 / math.sqrt(token_count)
    grad_norm = grad_norm * factor
    grad_qkv = grad_qkv * factor
    grad_attn = grad_attn * factor
    grad_up = grad_up * factor
    grad_down = grad_down * factor
    new_norm, new_mom_norm = adam_step(norm_params, grad_norm, mom_norm, 0.0)
    new_qkv, new_mom_qkv = adam_step(w_qkv, grad_qkv, mom_qkv, decay_rate)
    new_attn, new_mom_attn = adam_step(w_attn, grad_attn, mom_attn, decay_rate)
    new_up, new_mom_up = adam_step(w_up, grad_up, mom_up, decay_rate)
    new_down, new_mom_down = adam_step(w_down, grad_down, mom_down, decay_rate)
    return (
        block_out,
        input_grad,
        grad_norm,
        grad_qkv,
        grad_attn,
        grad_up,
        grad_down,
        new_norm,
        new_qkv,
        new_attn,
        new_up,
        new_down,
        new_mom_norm,
        new_mom_qkv,
        new_mom_attn,
        new_mom_up,
        new_mom_down,
    )


def solution(mesh):
    in_specs = (
        P(("dp", "row"), "col"),
        P(("dp", "row"), "col"),
        P(None, "col"),
        P(None, "row", "dp", "col"),
        P("row", "dp", "col"),
        P(("dp", "row"), "col"),
        P(("dp", "row"), "col"),
        P(None, None, "col"),
        P(None, None, "row", "dp", "col"),
        P(None, "row", "dp", "col"),
        P(None, ("dp", "row"), "col"),
        P(None, ("dp", "row"), "col"),
    )
    out_specs = (
        P(("dp", "row"), "col"),
        P(("dp", "row"), "col"),
        P(None, "col"),
        P(None, "row", "dp", "col"),
        P("row", "dp", "col"),
        P(("dp", "row"), "col"),
        P(("dp", "row"), "col"),
        P(None, "col"),
        P(None, "row", "dp", "col"),
        P("row", "dp", "col"),
        P(("dp", "row"), "col"),
        P(("dp", "row"), "col"),
        P(None, None, "col"),
        P(None, None, "row", "dp", "col"),
        P(None, "row", "dp", "col"),
        P(None, ("dp", "row"), "col"),
        P(None, ("dp", "row"), "col"),
    )
    return jax.shard_map(
        on_device, mesh=mesh, in_specs=in_specs, out_specs=out_specs, check_vma=False
    )
```

```python
import functools
import math

import jax
import jax.numpy as jnp
from jax import lax
from jax.experimental import pallas as pl
from jax.experimental.pallas import tpu as pltpu
from jax.sharding import PartitionSpec as P

SEQ = 512
STEP = 4
LOW = 2


norm_eps = 1e-05
adam_eps = 1e-08
beta_one = 0.9
beta_two = 0.95
learn_rate = 0.02
decay_rate = 0.1
gelu_coef = math.sqrt(2.0 / math.pi)
cubic_coef = 0.044715
masked_score = -1e30

group = ("row", "col")
swap_pair = [(0, 1), (1, 0)]
spread_first = [(1, 2), (2, 1)]
spread_second = [(0, 2), (3, 1), (1, 0), (2, 3)]
collect_second = [(dst, src) for src, dst in spread_second]


def smooth_pair(values):
    squared = values * values
    bent = jnp.tanh(gelu_coef * (values + cubic_coef * squared * values))
    smooth = 0.5 * values * (1.0 + bent)
    slope = 0.5 * (1.0 + bent) + 0.5 * values * (1.0 - bent * bent) * gelu_coef * (
        1.0 + 3.0 * cubic_coef * squared
    )
    return (smooth, slope)


def wide(left, right, dims):
    return lax.dot_general(left, right, (dims, ((), ())), preferred_element_type=jnp.float32)


def normalize(rows_in, gain_row, shift_row):
    count = rows_in.shape[1]
    mean_here = jnp.mean(rows_in, axis=1, keepdims=True)
    offset = rows_in - mean_here
    square_here = jnp.sum(offset * offset, axis=1, keepdims=True)
    there = lax.ppermute(jnp.concatenate([mean_here, square_here], axis=1), "col", swap_pair)
    gap = mean_here - there[:, :1]
    spread = (square_here + there[:, 1:] + gap * gap * (0.5 * count)) / (2.0 * count)
    inverse = lax.rsqrt(spread + norm_eps)
    normal = (rows_in - (mean_here - 0.5 * gap)) * inverse
    return (normal, inverse, (normal * gain_row + shift_row).astype(jnp.bfloat16))


def norm_back(grad_normed, normal, inverse, gain_row):
    count = 2.0 * grad_normed.shape[1]
    scaled = grad_normed * gain_row
    here = jnp.concatenate(
        [
            jnp.sum(scaled, axis=1, keepdims=True),
            jnp.sum(scaled * normal, axis=1, keepdims=True),
        ],
        axis=1,
    )
    total = (here + lax.ppermute(here, "col", swap_pair)) / count
    return inverse * (scaled - total[:, :1] - normal * total[:, 1:])


def pick(flag, one, other):
    return jnp.where(flag, one, other), jnp.where(flag, other, one)


def spread_rows(block):
    row, col = lax.axis_index("row"), lax.axis_index("col")
    first = lax.ppermute(block, group, spread_first)
    second = lax.ppermute(block, group, spread_second)
    first = jnp.where(row == col, block, first)
    low, high = pick(row == 0, first, second)
    return low, high


def collect_rows(low, high):
    row, col = lax.axis_index("row"), lax.axis_index("col")
    first, second = pick(row == 0, low, high)
    first_in = lax.ppermute(first.astype(jnp.bfloat16), group, spread_first)
    second_in = lax.ppermute(second.astype(jnp.bfloat16), group, collect_second)
    return jnp.where(row == col, first, first_in.astype(jnp.float32)) + second_in.astype(
        jnp.float32
    )


def out_project(rows, weight):
    half = weight.shape[1] // 2
    return collect_rows(
        wide(rows, weight[:, :half], ((1,), (0,))), wide(rows, weight[:, half:], ((1,), (0,)))
    )


def small_ring():
    size = lax.axis_size("dp")
    return size % LOW == 0 and size <= 8


def high_steps(sign):
    size = lax.axis_size("dp")
    high = size // LOW
    return [
        [(i, ((i // LOW + sign * step) % high) * LOW + i % LOW) for i in range(size)]
        for step in range(1, high)
    ]


def low_step():
    return [(i, i ^ 1) for i in range(lax.axis_size("dp"))]


def gather_near(shard, axis):
    shard = shard.astype(jnp.bfloat16)
    if not small_ring():
        return lax.all_gather(shard, "dp", axis=axis, tiled=True)
    return jnp.concatenate(
        [shard] + [lax.ppermute(shard, "dp", perm) for perm in high_steps(1)], axis=axis
    )


def gather_far(near, axis):
    block = near
    if small_ring():
        block = jnp.concatenate([near, lax.ppermute(near, "dp", low_step())], axis=axis)
    there = lax.ppermute(block, "col", swap_pair)
    low, high = pick(lax.axis_index("col") == 0, block, there)
    return jnp.concatenate([low, high], axis=-1)


def reduce_cols(own, away):
    return own + lax.ppermute(away, "col", swap_pair).astype(jnp.float32)


def halve(total, axis):
    if not small_ring():
        return total, total
    near, far = jnp.split(total, 2, axis=axis)
    return near, far.astype(jnp.bfloat16)


def reduce_low(near, far, axis):
    if not small_ring():
        return near, ()
    near = near + lax.ppermute(far, "dp", low_step()).astype(jnp.float32)
    own, *rest = jnp.split(near, lax.axis_size("dp") // LOW, axis=axis)
    return own, tuple(piece.astype(jnp.bfloat16) for piece in rest)


def reduce_high(own, rest, axis):
    if not small_ring():
        return lax.psum_scatter(own, "dp", scatter_dimension=axis, tiled=True)
    for piece, perm in zip(rest, high_steps(-1)):
        own = own + lax.ppermute(piece, "dp", perm).astype(jnp.float32)
    return own


def reduce_weight(make, axis):
    total = reduce_cols(make(True), make(False).astype(jnp.bfloat16))
    return reduce_high(*reduce_low(*halve(total, axis), axis), axis)


def sum_everywhere(terms):
    if not small_ring():
        return lax.psum(terms, ("dp", "row"))
    terms = terms + lax.ppermute(terms, "row", swap_pair)
    terms = terms + lax.ppermute(terms, "dp", low_step())
    moved = [lax.ppermute(terms, "dp", perm) for perm in high_steps(1)]
    for piece in moved:
        terms = terms + piece
    return terms


def head_scores(triples_ref, heads, size, head):
    width = heads * size
    query = triples_ref[:, head * size : (head + 1) * size]
    key = triples_ref[:, width + head * size : width + (head + 1) * size]
    value = triples_ref[:, 2 * width + head * size : 2 * width + (head + 1) * size]
    scores = wide(query, key, ((1,), (1,))) * (1.0 / math.sqrt(size))
    length = scores.shape[0]
    allowed = lax.broadcasted_iota(jnp.int32, (length, length), 0) >= lax.broadcasted_iota(
        jnp.int32, (length, length), 1
    )
    return query, key, value, jnp.where(allowed, scores, masked_score)


def attend_kernel(heads, size, triples_ref, mixed_ref, total_ref):
    for head in range(heads):
        _, _, value, scores = head_scores(triples_ref, heads, size, head)
        highest = jnp.max(scores, axis=1, keepdims=True)
        log_total = highest + jnp.log(jnp.sum(jnp.exp(scores - highest), axis=1, keepdims=True))
        probs = jnp.exp(scores - log_total).astype(jnp.bfloat16)
        mixed_ref[:, head * size : (head + 1) * size] = wide(probs, value, ((1,), (0,))).astype(
            jnp.bfloat16
        )
        total_ref[:, head : head + 1] = log_total


def attend_back_kernel(heads, size, triples_ref, grad_ref, total_ref, out_ref):
    width = heads * size
    scale = 1.0 / math.sqrt(size)
    for head in range(heads):
        query, key, value, scores = head_scores(triples_ref, heads, size, head)
        grad_mixed = grad_ref[:, head * size : (head + 1) * size]
        probs = jnp.exp(scores - total_ref[:, head : head + 1])
        grad_values = wide(probs.astype(jnp.bfloat16), grad_mixed, ((0,), (0,)))
        grad_probs = wide(grad_mixed, value, ((1,), (1,)))
        delta = jnp.sum(probs * grad_probs, axis=1, keepdims=True)
        grad_scores = (probs * (grad_probs - delta) * scale).astype(jnp.bfloat16)
        for part, piece in enumerate(
            (
                wide(grad_scores, key, ((1,), (0,))),
                wide(grad_scores, query, ((0,), (0,))),
                grad_values,
            )
        ):
            start = part * width + head * size
            out_ref[:, start : start + size] = piece.astype(jnp.bfloat16)


def by_sequence(kernel, operands, outs):
    rows = operands[0].shape[0]

    def spec(shape):
        return pl.BlockSpec((SEQ, shape[1]), lambda step: (step, 0))

    return pl.pallas_call(
        kernel,
        grid=(rows // SEQ,),
        in_specs=[spec(item.shape) for item in operands],
        out_specs=[spec(item.shape) for item in outs],
        out_shape=outs,
        compiler_params=pltpu.CompilerParams(vmem_limit_bytes=40 * 1024 * 1024),
        cost_estimate=pl.CostEstimate(
            flops=rows * SEQ * 2048, bytes_accessed=rows * 8192, transcendentals=rows * SEQ * 6
        ),
    )(*operands)


def adam_step(weight, grad, moments, decay):
    first_moment = beta_one * moments[0] + (1.0 - beta_one) * grad
    second_moment = beta_two * moments[1] + (1.0 - beta_two) * grad * grad
    step_size = (
        first_moment
        / (1.0 - beta_one**STEP)
        / (jnp.sqrt(second_moment / (1.0 - beta_two**STEP)) + adam_eps)
    )
    return (
        weight - learn_rate * (step_size + decay * weight),
        jnp.stack([first_moment, second_moment]),
    )


def on_device(
    block_in,
    upstream,
    norm_params,
    w_qkv,
    w_attn,
    w_up,
    w_down,
    mom_norm,
    mom_qkv,
    mom_attn,
    mom_up,
    mom_down,
):
    heads = w_qkv.shape[1]
    size = w_qkv.shape[2] * lax.axis_size("dp")
    width = heads * size
    at_low = lax.axis_index("col") == 0

    normal_one, inverse_one, normed_one = normalize(block_in, norm_params[0], norm_params[1])
    tie = lax.optimization_barrier
    one_low, one_high = spread_rows(normed_one)
    near_qkv = gather_near(w_qkv, 2)
    near_qkv, attn_b, up_b, down_b, upstream_b = tie(
        (near_qkv,)
        + tuple(item.astype(jnp.bfloat16) for item in (w_attn, w_up, w_down, upstream))
    )
    qkv_mat = gather_far(near_qkv, 2).reshape(3 * width, -1)
    attn_mat = gather_far(gather_near(attn_b, 1), 1).reshape(width, -1)
    up_mat = gather_far(gather_near(up_b, 0), 0)
    down_mat = gather_far(gather_near(down_b, 0), 0)
    up_low, up_high = spread_rows(upstream_b)

    triples = wide(
        jnp.concatenate([one_low, one_high], axis=1), qkv_mat, ((1,), (1,))
    ).astype(jnp.bfloat16)
    mixed, log_total = by_sequence(
        functools.partial(attend_kernel, heads, size),
        (triples,),
        (
            jax.ShapeDtypeStruct((triples.shape[0], width), jnp.bfloat16),
            jax.ShapeDtypeStruct((triples.shape[0], heads), jnp.float32),
        ),
    )
    middle = block_in + out_project(mixed, attn_mat)
    normal_two, inverse_two, normed_two = normalize(middle, norm_params[2], norm_params[3])
    two_low, two_high = spread_rows(normed_two)
    grad_hidden = wide(jnp.concatenate([up_low, up_high], axis=1), down_mat, ((1,), (1,)))
    hidden_pre = wide(jnp.concatenate([two_low, two_high], axis=1), up_mat, ((1,), (1,)))
    activated, slope = smooth_pair(hidden_pre)
    activated = activated.astype(jnp.bfloat16)
    grad_pre = (grad_hidden * slope).astype(jnp.bfloat16)
    grad_normed_two = out_project(grad_pre, up_mat)

    def products(left, low, high):
        own, away = pick(at_low, low, high)
        return lambda mine: wide(left, own if mine else away, ((0,), (0,)))

    make_down = products(activated, up_low, up_high)
    make_up = products(grad_pre, two_low, two_high)
    grad_normed_two, away_down, away_up = tie(
        (
            grad_normed_two,
            make_down(False).astype(jnp.bfloat16),
            make_up(False).astype(jnp.bfloat16),
        )
    )
    middle_grad = upstream + norm_back(grad_normed_two, normal_two, inverse_two, norm_params[2])
    middle_b, activated_late = tie((middle_grad.astype(jnp.bfloat16), activated))
    mid_low, mid_high = spread_rows(middle_b)
    near_down, far_down = halve(reduce_cols(make_down(True), away_down), 0)
    near_up, far_up = halve(reduce_cols(make_up(True), away_up), 0)
    mid_low, mid_high, far_down, far_up = tie((mid_low, mid_high, far_down, far_up))
    own_down, rest_down = reduce_low(near_down, far_down, 0)
    own_up, rest_up = reduce_low(near_up, far_up, 0)
    block_out = middle + out_project(activated_late, down_mat)
    grad_mixed = wide(
        jnp.concatenate([mid_low, mid_high], axis=1), attn_mat, ((1,), (1,))
    ).astype(jnp.bfloat16)

    def by_head(make, parts):
        return lambda mine: make(mine).reshape(*parts, heads, size, -1)

    grad_attn = reduce_weight(by_head(products(mixed, mid_low, mid_high), ()), 1)
    (grad_triples,) = by_sequence(
        functools.partial(attend_back_kernel, heads, size),
        (triples, grad_mixed, log_total),
        (jax.ShapeDtypeStruct(triples.shape, jnp.bfloat16),),
    )
    grad_qkv = reduce_weight(by_head(products(grad_triples, one_low, one_high), (3,)), 2)
    grad_normed_one = out_project(grad_triples, qkv_mat)
    grad_normed_one, rest_down, rest_up = tie((grad_normed_one, rest_down, rest_up))
    grad_down = reduce_high(own_down, rest_down, 0)
    grad_up = reduce_high(own_up, rest_up, 0)
    input_grad = middle_grad + norm_back(grad_normed_one, normal_one, inverse_one, norm_params[0])
    norm_terms = jnp.stack(
        [
            jnp.sum(grad_normed_one * normal_one, axis=0),
            jnp.sum(grad_normed_one, axis=0),
            jnp.sum(grad_normed_two * normal_two, axis=0),
            jnp.sum(grad_normed_two, axis=0),
        ]
    )
    grad_norm = sum_everywhere(norm_terms)
    token_count = block_in.shape[0] * lax.axis_size("dp") * lax.axis_size("row")
    factor = 1.0 / math.sqrt(token_count)
    grad_norm = grad_norm * factor
    grad_qkv = grad_qkv * factor
    grad_attn = grad_attn * factor
    grad_up = grad_up * factor
    grad_down = grad_down * factor
    new_norm, new_mom_norm = adam_step(norm_params, grad_norm, mom_norm, 0.0)
    new_qkv, new_mom_qkv = adam_step(w_qkv, grad_qkv, mom_qkv, decay_rate)
    new_attn, new_mom_attn = adam_step(w_attn, grad_attn, mom_attn, decay_rate)
    new_up, new_mom_up = adam_step(w_up, grad_up, mom_up, decay_rate)
    new_down, new_mom_down = adam_step(w_down, grad_down, mom_down, decay_rate)
    return (
        block_out,
        input_grad,
        grad_norm,
        grad_qkv,
        grad_attn,
        grad_up,
        grad_down,
        new_norm,
        new_qkv,
        new_attn,
        new_up,
        new_down,
        new_mom_norm,
        new_mom_qkv,
        new_mom_attn,
        new_mom_up,
        new_mom_down,
    )


def solution(mesh):
    in_specs = (
        P(("dp", "row"), "col"),
        P(("dp", "row"), "col"),
        P(None, "col"),
        P(None, "row", "dp", "col"),
        P("row", "dp", "col"),
        P(("dp", "row"), "col"),
        P(("dp", "row"), "col"),
        P(None, None, "col"),
        P(None, None, "row", "dp", "col"),
        P(None, "row", "dp", "col"),
        P(None, ("dp", "row"), "col"),
        P(None, ("dp", "row"), "col"),
    )
    out_specs = (
        P(("dp", "row"), "col"),
        P(("dp", "row"), "col"),
        P(None, "col"),
        P(None, "row", "dp", "col"),
        P("row", "dp", "col"),
        P(("dp", "row"), "col"),
        P(("dp", "row"), "col"),
        P(None, "col"),
        P(None, "row", "dp", "col"),
        P("row", "dp", "col"),
        P(("dp", "row"), "col"),
        P(("dp", "row"), "col"),
        P(None, None, "col"),
        P(None, None, "row", "dp", "col"),
        P(None, "row", "dp", "col"),
        P(None, ("dp", "row"), "col"),
        P(None, ("dp", "row"), "col"),
    )
    return jax.shard_map(
        on_device, mesh=mesh, in_specs=in_specs, out_specs=out_specs, check_vma=False
    )
```
